32 devices in a mesh: dp: 2 (over y), slab: 4 (over z), view: 4 (over x, core).
Axes of the slice: x: 2, y: 2, z: 4, core: 2. Of those that a mesh axis runs over, the one named last changes fastest.
Arguments:
- latent_feats: bfloat16 [2, 4, 16, 32, 256], P('dp', 'view', 'slab'), may hold values from -6 to 6
- conv_weight: bfloat16 [2304, 256], P(('dp', 'slab')), may hold values from -0.125 to 0.125
- kv_weight: bfloat16 [256, 1536], P(('dp', 'slab')), may hold values from -0.375 to 0.375
- stream: bfloat16 [2, 4, 16, 32, 768], P('dp', 'view', 'slab'), may hold values from -6 to 6
- queries: bfloat16 [2, 4, 16, 32, 768], P('dp', 'view', 'slab'), may hold values from -102 to 102
- norm_gain: float32 [768], replicated, may hold values from 0.1 to 1.9
- up_weight: bfloat16 [768, 3072], P(('dp', 'slab'), 'view'), may hold values from -0.21875 to 0.21875
- down_weight: bfloat16 [768, 3072], P(('dp', 'slab'), 'view'), may hold values from -0.109375 to 0.109375
- band_start: int32 [2, 4, 16, 4], P('dp', 'view', 'slab'), may hold values from 0 to 15, as said below
- band_end: int32 [2, 4, 16, 4], P('dp', 'view', 'slab'), may hold values from 1 to 16
- visibility: int32 [2, 4, 4], P('dp'), may hold values 0 or 1
Outputs:
- output: bfloat16 [2, 4, 16, 32, 768], P('dp', 'view', 'slab')
The draws below stay inside these ranges and needn't reach their ends.
Inputs may be any that keep to these rules, and one draw needn't show every extreme that they name: band_end - band_start lies in 1 to 4 and equals 4 for some rows in every draw; for a row r both bounds lie within rows (r // 4) * 4 - 1 to (r // 4 + 1) * 4 + 1, clipped to the grid.
All inputs are finite; a program needn't handle non-finite values. No bound on the sum of `visibility` on one device may be relied on, other than what follows from the above.
Results may differ from the reference program's by a relative error of at most 0.0085.
Values may be sent and summed in bfloat16 or wider, within the bound.
A program may use at most 64 MiB of HBM per device.

```python
import jax
import jax.numpy as jnp
from jax import lax

D = 768
HEADS = 12
HEAD_DIM = 64
FF = 3072
C = 256
ROWS_DEV = 4
HALO = 1
BAND = 4
COLS = 32
SCENES = 2
VIEWS = 4
HEIGHT = 16
UNIT_GROUPS = 4
FF_GROUP = 768
N_SLAB = 4


def band_pair(key):
    base_key = jax.random.fold_in(key, 7)
    key_length, key_offset = jax.random.split(base_key)
    full_shape = (SCENES, VIEWS, HEIGHT, VIEWS)
    row_ids = jnp.arange(HEIGHT, dtype=jnp.int32).reshape(1, 1, HEIGHT, 1)
    block_top = row_ids // ROWS_DEV * ROWS_DEV
    lowest = jnp.maximum(block_top - HALO, 0)
    highest = jnp.minimum(block_top + ROWS_DEV + HALO, HEIGHT)
    length = jax.random.randint(key_length, full_shape, 1, BAND + 1)
    view_ids = jnp.arange(VIEWS, dtype=jnp.int32).reshape(1, VIEWS, 1, 1)
    other_ids = jnp.arange(VIEWS, dtype=jnp.int32).reshape(1, 1, 1, VIEWS)
    forced = row_ids == (view_ids + 5 * other_ids) % HEIGHT
    length = jnp.where(forced, BAND, length)
    room_left = jnp.broadcast_to(highest - lowest - length + 1, full_shape)
    offset = jax.random.randint(key_offset, full_shape, 0, room_left)
    first_rows = jnp.broadcast_to(lowest, full_shape) + offset
    return (first_rows.astype(jnp.int32), (first_rows + length).astype(jnp.int32))


def draw_band_start(key, part):
    return band_pair(key)[0]


def draw_band_end(key, part):
    return band_pair(key)[1]


def draw_queries(key, part):
    full_shape = (SCENES, VIEWS, HEIGHT, COLS, D)
    key_base = jax.random.fold_in(jax.random.fold_in(key, 11), 0)
    values = jnp.clip(jax.random.normal(key_base, full_shape, jnp.float32), -6.0, 6.0)
    return values.astype(jnp.bfloat16)


def place_ends(values, own_key, least, top_value):
    spot = [jax.random.randint(jax.random.fold_in(own_key, axis), (), 0, length) for axis, length in enumerate(values.shape)]
    longest = values.shape.index(max(values.shape))
    neighbour = spot[:longest] + [(spot[longest] + 1) % values.shape[longest]] + spot[longest + 1:]
    return values.at[tuple(spot)].set(least).at[tuple(neighbour)].set(top_value)


def block_scale(own_key, shape, pieces, least, high):
    loudness = 1.0
    for axis_at, shards_of in pieces:
        steps = jax.random.uniform(jax.random.fold_in(jax.random.fold_in(own_key, 6), axis_at), (shards_of,), jnp.float32, least / len(pieces), high / len(pieces))
        loudness = loudness * jnp.repeat(jnp.exp(steps), shape[axis_at] // shards_of).reshape((-1,) + (1,) * (len(shape) - 1 - axis_at))
    return loudness


def bell_draw(own_key, dims, scale, most, cuts=(), held_as=jnp.bfloat16):
    array = scale * jax.random.normal(own_key, dims, jnp.float32)
    if cuts:
        array = array * block_scale(own_key, dims, cuts, -0.22, 0.18)
    return jnp.clip(array, -most, most).astype(held_as)


def setup_inputs(seed: int = 0) -> dict:
    seeds = jax.random.split(jax.random.key(seed), 12)
    latent_feats = bell_draw(seeds[0], (SCENES, VIEWS, HEIGHT, COLS, C), 1.0, 6.0, ((0, 2), (1, 4), (2, 4)))
    conv_weight = bell_draw(seeds[1], (9 * C, C), (9 * C) ** -0.5, 0.125, ((0, 8),))
    kv_weight = bell_draw(seeds[2], (C, 2 * D), C ** -0.5, 0.375, ((0, 8),))
    stream = bell_draw(seeds[3], (SCENES, VIEWS, HEIGHT, COLS, D), 1.0, 6.0, ((0, 2), (1, 4), (2, 4)))
    queries = draw_queries(jax.random.fold_in(seeds[11], 71), 0)
    norm_gain = jnp.clip(1.0 + 0.18 * jax.random.normal(seeds[5], (D,), jnp.float32), 0.1, 1.9)
    up_weight = bell_draw(seeds[6], (D, FF), D ** -0.5, 0.21875, ((0, 8), (1, 4)))
    down_weight = bell_draw(seeds[7], (D, FF), FF ** -0.5, 0.109375, ((0, 8), (1, 4)))
    band_start = draw_band_start(jax.random.fold_in(seeds[11], 71), 0)
    band_end = draw_band_end(jax.random.fold_in(seeds[11], 71), 0)
    visibility = place_ends((jax.random.randint(seeds[10], (SCENES, VIEWS, VIEWS), 0, 2) < 1).astype(jnp.int32), jax.random.fold_in(seeds[10], 1), 0, 1)
    return {"latent_feats": latent_feats, "conv_weight": conv_weight, "kv_weight": kv_weight, "stream": stream, "queries": queries, "norm_gain": norm_gain, "up_weight": up_weight, "down_weight": down_weight, "band_start": band_start, "band_end": band_end, "visibility": visibility}


def conv_layer(view_feats, conv_weight):
    height, col_count, channels = view_feats.shape
    padded = jnp.pad(view_feats, ((1, 1), (1, 1), (0, 0)))
    running = jnp.zeros((height * col_count, channels), jnp.float32)
    for tap_index in range(9):
        row_off = tap_index // 3
        col_off = tap_index % 3
        window = padded[row_off:row_off + height, col_off:col_off + col_count].reshape(-1, channels)
        taps = conv_weight[tap_index * channels:(tap_index + 1) * channels]
        running = running + jnp.dot(window, taps, preferred_element_type=jnp.float32)
    summed = view_feats.reshape(-1, channels).astype(jnp.float32) + jax.nn.silu(running)
    return summed.astype(jnp.bfloat16).reshape(height, col_count, channels)

def band_attention(query_rows, near_kv, block_starts, block_ends, vis_row, view_id, first_row):
    near_rows = near_kv.shape[1]
    keys = near_kv[..., :D].reshape(-1, HEADS, HEAD_DIM).astype(jnp.float32)
    values = near_kv[..., D:].reshape(-1, HEADS, HEAD_DIM).astype(jnp.float32)
    key_rows = first_row - HALO + jnp.arange(near_rows, dtype=jnp.int32)
    inside = (block_starts[:, :, None] <= key_rows) & (key_rows < block_ends[:, :, None])
    seen = (jnp.arange(VIEWS, dtype=jnp.int32) == view_id) | (vis_row == 1)
    allowed = inside & seen[None, :, None]
    allowed = jnp.broadcast_to(allowed[:, None, :, :, None], (ROWS_DEV, COLS, VIEWS, near_rows, COLS))
    allowed = allowed.reshape(ROWS_DEV * COLS, -1)
    query_heads = query_rows.reshape(-1, HEADS, HEAD_DIM).astype(jnp.float32)
    scores = jnp.einsum('qhd,khd->hqk', query_heads, keys) * HEAD_DIM ** (-0.5)
    scores = jnp.where(allowed[None], scores, -1e+30)
    highest = lax.optimization_barrier(jnp.max(scores, axis=-1, keepdims=True))
    weights = jnp.exp(scores - highest)
    weights = weights / lax.optimization_barrier(jnp.sum(weights, axis=-1, keepdims=True))
    probs = lax.optimization_barrier(weights.astype(jnp.bfloat16)).astype(jnp.float32)
    return jnp.einsum('hqk,khd->qhd', probs, values).reshape(-1, D)

def reference(latent_feats, conv_weight, kv_weight, stream, queries, norm_gain, up_weight, down_weight, band_start, band_end, visibility):

    def scene_pass(operands):
        scene_feats, scene_stream, scene_queries, scene_starts, scene_ends, scene_visible = operands
        encoded = jnp.stack([conv_layer(scene_feats[view_index], conv_weight) for view_index in range(VIEWS)])
        projected = jnp.dot(encoded.reshape(-1, C), kv_weight, preferred_element_type=jnp.float32)
        projected = projected.astype(jnp.bfloat16).reshape(VIEWS, HEIGHT, COLS, 2 * D)
        padded = jnp.pad(projected, ((0, 0), (HALO, HALO), (0, 0), (0, 0)))

        def block_pass(block_index):
            view_id = (block_index // N_SLAB).astype(jnp.int32)
            first_row = (block_index % N_SLAB * ROWS_DEV).astype(jnp.int32)
            near_kv = lax.dynamic_slice_in_dim(padded, first_row, ROWS_DEV + 2 * HALO, 1)
            view_queries = lax.dynamic_index_in_dim(scene_queries, view_id, 0, False)
            query_rows = lax.dynamic_slice_in_dim(view_queries, first_row, ROWS_DEV, 0).reshape(-1, D)
            view_starts = lax.dynamic_index_in_dim(scene_starts, view_id, 0, False)
            view_ends = lax.dynamic_index_in_dim(scene_ends, view_id, 0, False)
            block_starts = lax.dynamic_slice_in_dim(view_starts, first_row, ROWS_DEV, 0)
            block_ends = lax.dynamic_slice_in_dim(view_ends, first_row, ROWS_DEV, 0)
            vis_row = lax.dynamic_index_in_dim(scene_visible, view_id, 0, False)
            return band_attention(query_rows, near_kv, block_starts, block_ends, vis_row, view_id, first_row)
        attended = lax.map(block_pass, jnp.arange(VIEWS * N_SLAB, dtype=jnp.int32))
        attended = attended.reshape(VIEWS * HEIGHT * COLS, D)
        residual = scene_stream.reshape(-1, D).astype(jnp.float32) + attended
        square_mean = lax.optimization_barrier(jnp.mean(residual * residual, axis=-1, keepdims=True))
        normed = (residual * lax.rsqrt(square_mean + 1e-06) * norm_gain).astype(jnp.bfloat16)
        hidden = jax.nn.gelu(jnp.dot(normed, up_weight, preferred_element_type=jnp.float32), approximate=True)
        hidden = hidden.astype(jnp.bfloat16)
        mixed = jnp.zeros((VIEWS * HEIGHT * COLS, D), jnp.float32)
        for group_index in range(UNIT_GROUPS):
            lower = group_index * FF_GROUP
            term = lax.dot_general(hidden[:, lower:lower + FF_GROUP], down_weight[:, lower:lower + FF_GROUP], (((1,), (1,)), ((), ())), preferred_element_type=jnp.float32)
            term = lax.optimization_barrier(term.astype(jnp.bfloat16))
            mixed = mixed + term.astype(jnp.float32)
        return (residual + mixed).astype(jnp.bfloat16).reshape(VIEWS, HEIGHT, COLS, D)
    return lax.map(scene_pass, (latent_feats, stream, queries, band_start, band_end, visibility))
```

```python
import jax
import jax.numpy as jnp
from jax import lax
from jax.experimental import pallas as pl
from jax.experimental.pallas import tpu as pltpu
from jax.sharding import PartitionSpec as P

HEAD_DIM = 64
HALO = 1
MESH = pl.DeviceIdType.MESH
CONV, KV, UP, DOWN = range(4)


def block_kernel(
    n_dp, n_slab, n_view, gather, row_count, col_count,
    feats, conv_in, kv_in, stream, queries, gain, up_in, down_in,
    starts, ends, visible,
    out,
    conv_buf, kv_buf, up_buf, down_buf, feat_buf, enc_buf, proj_buf, bias_buf,
    stream_buf, query_buf, gain_buf, res_buf, tokens, terms, sums,
    loc_sem, z_send, z_recv, y_send, y_recv, c_send, c_recv, f_send, f_recv,
    t_send, t_recv, s_send, s_recv,
):
    d = lax.axis_index("dp")
    s = lax.axis_index("slab")
    v = lax.axis_index("view")
    tokens_dev = row_count * col_count
    channels = feats.shape[1]
    width = stream.shape[1]
    edge = (HALO + 1) * col_count
    near = row_count + 2 * HALO
    half_id = lax.rem(v, 2)
    partner = v + 1 - 2 * half_id

    def view_at(i):
        chip = lax.rem(v // 2 + i // 2, n_view // 2)
        return chip * 2 + lax.rem(half_id + i % 2, 2)

    barrier = pltpu.get_barrier_semaphore()

    def hello(**where):
        pl.semaphore_signal(barrier, inc=1, device_id=where, device_id_type=MESH)

    greeted = n_view - 1
    for i in range(1, n_view):
        hello(view=view_at(i))
    side_views = range(n_view)
    if gather:
        side_views = range(1, n_view)
        greeted += n_slab - 1 + n_dp - 1
        for o in range(1, n_slab):
            hello(slab=lax.rem(s + o, n_slab))
        for i in range(1, n_dp):
            hello(dp=lax.rem(d + i, n_dp))

    @pl.when(s > 0)
    def _():
        for i in side_views:
            hello(slab=s - 1, view=view_at(i))

    @pl.when(s < n_slab - 1)
    def _():
        for i in side_views:
            hello(slab=s + 1, view=view_at(i))

    sides = jnp.where(s > 0, 1, 0) + jnp.where(s < n_slab - 1, 1, 0)
    pl.semaphore_wait(barrier, greeted + len(side_views) * sides)

    bufs = (conv_buf, kv_buf, up_buf, down_buf)
    srcs = (conv_in, kv_in, up_in, down_in)
    sends = []

    def region(w, i, o, other=False):
        rows = srcs[w].shape[0]
        k = lax.rem(d - i + n_dp, n_dp) * n_slab + lax.rem(s - o + n_slab, n_slab)
        at = pl.ds(pl.multiple_of(k * rows, 16), rows)
        if w in (UP, DOWN):
            return bufs[w].at[at]
        half = bufs[w].shape[1] // 2
        side = 1 - half_id if other else half_id
        return bufs[w].at[at, pl.ds(pl.multiple_of(side * half, 128), half)]

    def own_part(w):
        if w in (UP, DOWN):
            return srcs[w]
        half = bufs[w].shape[1] // 2
        return srcs[w].at[:, pl.ds(pl.multiple_of(half_id * half, 128), half)]

    def push(src, dst, send_sem, recv_sem, **where):
        copy = pltpu.make_async_remote_copy(
            src_ref=src, dst_ref=dst, send_sem=send_sem, recv_sem=recv_sem,
            device_id=where, device_id_type=MESH,
        )
        copy.start()
        sends.append(copy)

    def landed(dst, send_sem, recv_sem, **where):
        pltpu.make_async_remote_copy(
            src_ref=dst, dst_ref=dst, send_sem=send_sem, recv_sem=recv_sem,
            device_id=where, device_id_type=MESH,
        ).wait_recv()

    def send_z(w):
        for o in range(1, n_slab):
            push(own_part(w), region(w, 0, 0), z_send.at[w, o], z_recv.at[w, o],
                 slab=lax.rem(s + o, n_slab))

    def send_y(w):
        for i in range(1, n_dp):
            push(own_part(w), region(w, 0, 0), y_send.at[w, i, 0], y_recv.at[w, i, 0],
                 dp=lax.rem(d + i, n_dp))

    def to_core(w, i, o):
        if w in (CONV, KV):
            push(region(w, i, o), region(w, i, o), c_send.at[w, i, o], c_recv.at[w, i, o],
                 view=partner)

    def relay_z(w, o):
        landed(region(w, 0, o), z_send.at[w, o], z_recv.at[w, o],
               slab=lax.rem(s - o + n_slab, n_slab))
        for i in range(1, n_dp):
            push(region(w, 0, o), region(w, 0, o), y_send.at[w, i, o], y_recv.at[w, i, o],
                 dp=lax.rem(d + i, n_dp))
        to_core(w, 0, o)

    def take_y(w, o):
        for i in range(1, n_dp):
            landed(region(w, i, o), y_send.at[w, i, o], y_recv.at[w, i, o],
                   dp=lax.rem(d - i + n_dp, n_dp))
            to_core(w, i, o)

    def take_core(w):
        for i in range(n_dp):
            for o in range(n_slab):
                if i or o:
                    landed(region(w, i, o, True), c_send.at[w, i, o], c_recv.at[w, i, o],
                           view=partner)

    def local(src, dst, index):
        copy = pltpu.make_async_copy(src, dst, loc_sem.at[index])
        copy.start()
        return copy

    if gather:
        send_z(CONV)
        send_y(CONV)

    low = pl.ds(0, edge)
    mid = pl.ds(edge, tokens_dev)
    high = pl.ds(edge + tokens_dev, edge)

    def feat_copy(i, part):
        u = view_at(i)
        if part == 0:
            return pltpu.make_async_remote_copy(
                feats, feat_buf.at[v, mid], f_send.at[i, 0], f_recv.at[i, 0],
                device_id={"view": u}, device_id_type=MESH)
        if part == 1:
            return pltpu.make_async_remote_copy(
                feats.at[pl.ds(tokens_dev - edge, edge)], feat_buf.at[v, low],
                f_send.at[i, 1], f_recv.at[i, 1],
                device_id={"slab": s + 1, "view": u}, device_id_type=MESH)
        return pltpu.make_async_remote_copy(
            feats.at[pl.ds(0, edge)], feat_buf.at[v, high],
            f_send.at[i, 2], f_recv.at[i, 2],
            device_id={"slab": s - 1, "view": u}, device_id_type=MESH)

    own_feat = local(feats, feat_buf.at[v, mid], 0)

    def source_view(i):
        chip = lax.rem(v // 2 - i // 2 + n_view // 2, n_view // 2)
        return chip * 2 + lax.rem(half_id + i % 2, 2)

    def feat_landed(i, part):
        where = (mid, low, high)[part]
        ref = feat_buf.at[source_view(i), where]
        landed(ref, f_send.at[i, part], f_recv.at[i, part], view=source_view(1))

    for i in range(1, n_view):
        feat_copy(i, 0).start()

    @pl.when(s < n_slab - 1)
    def _():
        for i in range(n_view):
            feat_copy(i, 1).start()

    @pl.when(s > 0)
    def _():
        for i in range(n_view):
            feat_copy(i, 2).start()

    if gather:
        send_z(KV)
        send_y(KV)
    loads = [
        local(stream, stream_buf, 1),
        local(queries, query_buf, 2),
        local(gain, gain_buf, 3),
    ]
    if gather:
        weight_loads = []
        for w in range(4):
            rows = srcs[w].shape[0]
            at = pl.ds(pl.multiple_of((d * n_slab + s) * rows, 16), rows)
            weight_loads.append(local(srcs[w], bufs[w].at[at], 4 + w))
    else:
        weight_loads = [local(srcs[w], bufs[w], 4 + w) for w in range(4)]

    @pl.when(s == 0)
    def _():
        feat_buf[:, 0:edge, :] = jnp.zeros((n_view, edge, channels), jnp.bfloat16)

    @pl.when(s == n_slab - 1)
    def _():
        feat_buf[:, edge + tokens_dev:, :] = jnp.zeros((n_view, edge, channels), jnp.bfloat16)

    k_count = n_view * near * col_count
    lane = lax.broadcasted_iota(jnp.int32, (1, k_count), 1)
    key_view = jnp.zeros((1, k_count), jnp.int32)
    key_row = jnp.zeros((1, k_count), jnp.int32)
    for b in range(1, n_view * near):
        key_row = key_row + jnp.where(lane >= b * col_count, 1, 0)
    for b in range(1, n_view):
        key_view = key_view + jnp.where(lane >= b * near * col_count, 1, 0)
    key_row = key_row - near * key_view + (s * row_count - HALO)
    seen = jnp.zeros((1, k_count), jnp.int32)
    for u in range(n_view):
        flag = jnp.where(v == u, 1, visible[0, v, u])
        seen = jnp.where(key_view == u, flag, seen)
    for r in range(row_count):
        first = jnp.zeros((1, k_count), jnp.int32)
        last = jnp.zeros((1, k_count), jnp.int32)
        for u in range(n_view):
            first = jnp.where(key_view == u, starts[0, 0, r, u], first)
            last = jnp.where(key_view == u, ends[0, 0, r, u], last)
        fits = jnp.where(key_row >= first, 1, 0) * jnp.where(key_row < last, 1, 0)
        fits = fits * jnp.where(seen == 1, 1, 0)
        addend = jnp.where(fits == 1, 0.0, -1e30)
        bias_buf[r * col_count:(r + 1) * col_count, :] = jnp.broadcast_to(
            addend, (col_count, k_count))

    if gather:
        take_y(CONV, 0)
        for o in range(1, n_slab):
            relay_z(CONV, o)
        send_z(UP)
        send_y(UP)
        take_y(KV, 0)
        for o in range(1, n_slab):
            relay_z(KV, o)
        for o in range(1, n_slab):
            take_y(CONV, o)
        send_z(DOWN)
        send_y(DOWN)
        for o in range(1, n_slab):
            take_y(KV, o)
    own_feat.wait()
    for i in range(1, n_view):
        feat_landed(i, 0)

    @pl.when(s > 0)
    def _():
        for i in range(n_view):
            feat_landed(i, 1)

    @pl.when(s < n_slab - 1)
    def _():
        for i in range(n_view):
            feat_landed(i, 2)

    weight_loads[CONV].wait()
    if gather:
        take_core(CONV)

    span = near * col_count
    count = (row_count + 2 * (HALO + 1)) * col_count
    column = lax.broadcasted_iota(jnp.int32, (count, channels), 0) & (col_count - 1)
    for u in range(n_view):
        x = feat_buf[u]
        wide = x.astype(jnp.float32)
        before = jnp.where(column == 0, 0.0, pltpu.roll(wide, 1, 0)).astype(jnp.bfloat16)
        after = jnp.where(column == col_count - 1, 0.0, pltpu.roll(wide, count - 1, 0)).astype(
            jnp.bfloat16)
        taps = [
            part[row * col_count:row * col_count + span]
            for row in range(3) for part in (before, x, after)
        ]
        running = jnp.dot(jnp.concatenate(taps, axis=1), conv_buf[...],
                          preferred_element_type=jnp.float32)
        gated = running / (1.0 + jnp.exp(-running))
        enc_buf[u * span:(u + 1) * span, :] = (
            wide[HALO * col_count:HALO * col_count + span] + gated).astype(jnp.bfloat16)

    weight_loads[KV].wait()
    if gather:
        take_core(KV)
    for u in range(n_view):
        proj_buf[u * span:(u + 1) * span, :] = jnp.dot(
            enc_buf[u * span:(u + 1) * span, :], kv_buf[...],
            preferred_element_type=jnp.float32).astype(jnp.bfloat16)

    for copy in loads:
        copy.wait()

    per = 256 // HEAD_DIM
    head_of = lax.broadcasted_iota(jnp.int32, (tokens_dev, per * HEAD_DIM), 1) // HEAD_DIM
    total = jnp.zeros((tokens_dev, 1), jnp.float32)
    for g in range(width // (per * HEAD_DIM)):
        if gather and g + 1 < n_slab:
            relay_z(UP, g + 1)
        at = slice(g * per * HEAD_DIM, (g + 1) * per * HEAD_DIM)
        query = query_buf[:, at] * jnp.bfloat16(HEAD_DIM ** -0.5)
        stack = jnp.concatenate(
            [jnp.where(head_of == h, query, jnp.bfloat16(0)) for h in range(per)], axis=0)
        scores = lax.dot_general(stack, proj_buf[:, at], (((1,), (1,)), ((), ())),
                                 preferred_element_type=jnp.float32)
        value = proj_buf[:, width + g * per * HEAD_DIM:width + (g + 1) * per * HEAD_DIM]
        attended = jnp.zeros((tokens_dev, per * HEAD_DIM), jnp.float32)
        for h in range(per):
            part = scores[h * tokens_dev:(h + 1) * tokens_dev] + bias_buf[...]
            weights = jnp.exp(part - jnp.max(part, axis=1, keepdims=True))
            inverse = 1.0 / jnp.sum(weights, axis=1, keepdims=True)
            probs = (weights * inverse).astype(jnp.bfloat16)
            mixed = jnp.dot(probs, value, preferred_element_type=jnp.float32)
            attended = jnp.where(head_of == h, mixed, attended)
        residual = stream_buf[:, at].astype(jnp.float32) + attended
        res_buf[:, at] = residual
        total = total + jnp.sum(residual * residual, axis=1, keepdims=True)
    scale = lax.rsqrt(total * (1.0 / width) + 1e-06)
    tokens[v] = (res_buf[...] * scale * gain_buf[...]).astype(jnp.bfloat16)
    for i in range(1, n_view):
        push(tokens.at[v], tokens.at[v], t_send.at[i], t_recv.at[i], view=view_at(i))
    if gather:
        for o in range(width // (per * HEAD_DIM) + 1, n_slab):
            relay_z(UP, o)
        for o in range(1, n_slab):
            relay_z(DOWN, o)
        for o in range(n_slab):
            take_y(UP, o)
    weight_loads[UP].wait()

    def unit(u):
        return jax.nn.gelu(
            jnp.dot(tokens[u], up_buf[...], preferred_element_type=jnp.float32),
            approximate=True).astype(jnp.bfloat16)

    def term(hidden):
        return lax.dot_general(hidden, down_buf[...], (((1,), (1,)), ((), ())),
                               preferred_element_type=jnp.float32).astype(jnp.bfloat16)

    own_hidden = unit(v)
    for i in range(1, n_view):
        u = source_view(i)
        landed(tokens.at[u], t_send.at[i], t_recv.at[i], view=u)
        hidden = unit(u)
        if i == 1:
            weight_loads[DOWN].wait()
            if gather:
                for o in range(n_slab):
                    take_y(DOWN, o)
        terms[i] = term(hidden)
        push(terms.at[i], sums.at[i], s_send.at[i], s_recv.at[i], view=u)
    mixed = term(own_hidden).astype(jnp.float32)
    for i in range(1, n_view):
        landed(sums.at[i], s_send.at[i], s_recv.at[i], view=view_at(i))
        mixed = mixed + sums[i].astype(jnp.float32)
    out[...] = (res_buf[...] + mixed).astype(jnp.bfloat16)

    for copy in sends:
        copy.wait_send()
    for i in range(1, n_view):
        feat_copy(i, 0).wait_send()

    @pl.when(s < n_slab - 1)
    def _():
        for i in range(n_view):
            feat_copy(i, 1).wait_send()

    @pl.when(s > 0)
    def _():
        for i in range(n_view):
            feat_copy(i, 2).wait_send()


def solution(mesh):
    n_dp, n_slab, n_view = (mesh.shape[name] for name in ("dp", "slab", "view"))

    def shards(
        latent_feats, conv_weight, kv_weight, stream, queries, norm_gain,
        up_weight, down_weight, band_start, band_end, visibility,
    ):
        row_count, col_count, channels = latent_feats.shape[2:]
        width = stream.shape[4]
        units = up_weight.shape[1]
        tokens = row_count * col_count
        group = n_dp * n_slab
        weights = [conv_weight, kv_weight, up_weight, down_weight]
        gather = all(w.shape[0] % 16 == 0 for w in weights)
        if not gather:
            weights = [lax.all_gather(w, ("dp", "slab"), axis=0, tiled=True) for w in weights]
        near = row_count + 2 * HALO
        count = row_count + 2 * (HALO + 1)
        keys = n_view * near * col_count

        def kernel(*refs):
            block_kernel(n_dp, n_slab, n_view, gather, row_count, col_count, *refs)

        anywhere = pl.BlockSpec(memory_space=pl.ANY)
        scalar = pl.BlockSpec(memory_space=pltpu.SMEM)
        half = jnp.bfloat16
        dma = pltpu.SemaphoreType.DMA
        result = pl.pallas_call(
            kernel,
            out_shape=jax.ShapeDtypeStruct((tokens, width), half),
            in_specs=[anywhere] * 8 + [scalar] * 3,
            out_specs=pl.BlockSpec(memory_space=pltpu.VMEM),
            scratch_shapes=[
                pltpu.VMEM((9 * channels, channels), half),
                pltpu.VMEM((channels, 2 * width), half),
                pltpu.VMEM((width, units), half),
                pltpu.VMEM((width, units), half),
                pltpu.VMEM((n_view, count * col_count, channels), half),
                pltpu.VMEM((keys, channels), half),
                pltpu.VMEM((keys, 2 * width), half),
                pltpu.VMEM((tokens, keys), jnp.float32),
                pltpu.VMEM((tokens, width), half),
                pltpu.VMEM((tokens, width), half),
                pltpu.VMEM((1, width), jnp.float32),
                pltpu.VMEM((tokens, width), jnp.float32),
                pltpu.VMEM((n_view, tokens, width), half),
                pltpu.VMEM((n_view, tokens, width), half),
                pltpu.VMEM((n_view, tokens, width), half),
                dma((8,)),
                dma((4, n_slab)), dma((4, n_slab)),
                dma((4, n_dp, n_slab)), dma((4, n_dp, n_slab)),
                dma((2, n_dp, n_slab)), dma((2, n_dp, n_slab)),
                dma((n_view, 3)), dma((n_view, 3)),
                dma((n_view,)), dma((n_view,)),
                dma((n_view,)), dma((n_view,)),
            ],
            compiler_params=pltpu.CompilerParams(collective_id=0, has_side_effects=True),
        )(
            latent_feats.reshape(tokens, channels), weights[0], weights[1],
            stream.reshape(tokens, width), queries.reshape(tokens, width),
            norm_gain.reshape(1, width), weights[2], weights[3],
            band_start, band_end, visibility,
        )
        return result.reshape(1, 1, row_count, col_count, width)

    return jax.shard_map(
        shards,
        mesh=mesh,
        in_specs=(
            P("dp", "view", "slab", None, None),
            P(("dp", "slab"), None),
            P(("dp", "slab"), None),
            P("dp", "view", "slab", None, None),
            P("dp", "view", "slab", None, None),
            P(),
            P(("dp", "slab"), "view"),
            P(("dp", "slab"), "view"),
            P("dp", "view", "slab", None),
            P("dp", "view", "slab", None),
            P("dp", None, None),
        ),
        out_specs=P("dp", "view", "slab", None, None),
        check_vma=False,
    )
```

```python
import jax
import jax.numpy as jnp
from jax import lax
from jax.experimental import pallas as pl
from jax.experimental.pallas import tpu as pltpu
from jax.sharding import PartitionSpec as P

HEAD_DIM = 64
HALO = 1
MESH = pl.DeviceIdType.MESH
CONV, KV, UP, DOWN = range(4)


def block_kernel(
    n_dp, n_slab, n_view, gather, row_count, col_count,
    feats, conv_in, kv_in, stream, queries, gain, up_in, down_in,
    starts, ends, visible,
    out,
    conv_buf, kv_buf, up_buf, down_buf, feat_buf, enc_buf, proj_buf, bias_buf,
    stream_buf, query_buf, gain_buf, res_buf, tokens, terms, sums,
    loc_sem, z_send, z_recv, y_send, y_recv, c_send, c_recv, f_send, f_recv,
    t_send, t_recv, s_send, s_recv,
):
    d = lax.axis_index("dp")
    s = lax.axis_index("slab")
    v = lax.axis_index("view")
    tokens_dev = row_count * col_count
    channels = feats.shape[1]
    width = stream.shape[1]
    edge = (HALO + 1) * col_count
    near = row_count + 2 * HALO
    half_id = lax.rem(v, 2)
    partner = v + 1 - 2 * half_id

    def view_at(i):
        chip = lax.rem(v // 2 + i // 2, n_view // 2)
        return chip * 2 + lax.rem(half_id + i % 2, 2)

    barrier = pltpu.get_barrier_semaphore()

    def hello(**where):
        pl.semaphore_signal(barrier, inc=1, device_id=where, device_id_type=MESH)

    greeted = n_view - 1
    for i in range(1, n_view):
        hello(view=view_at(i))
    side_views = range(n_view)
    if gather:
        side_views = range(1, n_view)
        greeted += n_slab - 1 + n_dp - 1
        for o in range(1, n_slab):
            hello(slab=lax.rem(s + o, n_slab))
        for i in range(1, n_dp):
            hello(dp=lax.rem(d + i, n_dp))

    @pl.when(s > 0)
    def _():
        for i in side_views:
            hello(slab=s - 1, view=view_at(i))

    @pl.when(s < n_slab - 1)
    def _():
        for i in side_views:
            hello(slab=s + 1, view=view_at(i))

    sides = jnp.where(s > 0, 1, 0) + jnp.where(s < n_slab - 1, 1, 0)
    pl.semaphore_wait(barrier, greeted + len(side_views) * sides)

    bufs = (conv_buf, kv_buf, up_buf, down_buf)
    srcs = (conv_in, kv_in, up_in, down_in)
    sends = []

    def region(w, i, side, hop, other=False):
        rows = srcs[w].shape[0]
        k = lax.rem(d - i + n_dp, n_dp) * n_slab + s + (hop if side else -hop)
        at = pl.ds(pl.multiple_of(k * rows, 16), rows)
        if w in (UP, DOWN):
            return bufs[w].at[at]
        half = bufs[w].shape[1] // 2
        where = 1 - half_id if other else half_id
        return bufs[w].at[at, pl.ds(pl.multiple_of(where * half, 128), half)]

    def own_part(w):
        if w in (UP, DOWN):
            return srcs[w]
        half = bufs[w].shape[1] // 2
        return srcs[w].at[:, pl.ds(pl.multiple_of(half_id * half, 128), half)]

    def only(cond, action):
        if cond is None:
            action()
        else:
            pl.when(cond)(action)

    def push(cond, src, dst, send_sem, recv_sem, **where):
        def copy():
            return pltpu.make_async_remote_copy(
                src_ref=src(), dst_ref=dst(), send_sem=send_sem, recv_sem=recv_sem,
                device_id=where, device_id_type=MESH,
            )

        only(cond, lambda: copy().start())
        sends.append((cond, copy))

    def landed(cond, dst, send_sem, recv_sem, **where):
        only(cond, lambda: pltpu.make_async_remote_copy(
            src_ref=dst(), dst_ref=dst(), send_sem=send_sem, recv_sem=recv_sem,
            device_id=where, device_id_type=MESH,
        ).wait_recv())

    def there(side, hop):
        if hop == 0:
            return None
        return s + hop < n_slab if side else s >= hop

    def pass_z(w, side, hop, src):
        if hop + 1 >= n_slab:
            return
        cond = s > 0 if side else s < n_slab - 1
        if hop:
            cond = jnp.logical_and(cond, there(side, hop))
        push(cond, src, lambda: region(w, 0, side, hop),
             z_send.at[w, side, hop + 1], z_recv.at[w, side, hop + 1],
             slab=s - 1 if side else s + 1)

    def pass_y(w, side, hop, src):
        for i in range(1, n_dp):
            push(there(side, hop), src, lambda: region(w, 0, side, hop),
                 y_send.at[w, i, side, hop], y_recv.at[w, i, side, hop],
                 dp=lax.rem(d + i, n_dp))

    def to_core(w, i, side, hop):
        if w in (CONV, KV):
            part = lambda: region(w, i, side, hop)
            push(there(side, hop), part, part, c_send.at[w, i, side, hop],
                 c_recv.at[w, i, side, hop], view=partner)

    def send_own(w):
        pass_z(w, 0, 0, lambda: own_part(w))
        pass_z(w, 1, 0, lambda: own_part(w))
        pass_y(w, 0, 0, lambda: own_part(w))

    def relay_z(w, hop):
        for side in range(2):
            part = lambda side=side: region(w, 0, side, hop)
            landed(there(side, hop), part, z_send.at[w, side, hop], z_recv.at[w, side, hop],
                   slab=s + 1 if side else s - 1)
            pass_z(w, side, hop, part)
            pass_y(w, side, hop, part)
            to_core(w, 0, side, hop)

    def take_y(w, hop):
        for i in range(1, n_dp):
            for side in range(2 if hop else 1):
                landed(there(side, hop), lambda: region(w, i, side, hop),
                       y_send.at[w, i, side, hop], y_recv.at[w, i, side, hop],
                       dp=lax.rem(d - i + n_dp, n_dp))
                to_core(w, i, side, hop)

    def take_core(w):
        for i in range(n_dp):
            for hop in range(n_slab):
                for side in range(2 if hop else 1):
                    if i or hop:
                        landed(there(side, hop), lambda: region(w, i, side, hop, True),
                               c_send.at[w, i, side, hop], c_recv.at[w, i, side, hop],
                               view=partner)

    def local(src, dst, index):
        copy = pltpu.make_async_copy(src, dst, loc_sem.at[index])
        copy.start()
        return copy

    if gather:
        send_own(CONV)

    low = pl.ds(0, edge)
    mid = pl.ds(edge, tokens_dev)
    high = pl.ds(edge + tokens_dev, edge)

    def feat_copy(i, part):
        u = view_at(i)
        if part == 0:
            return pltpu.make_async_remote_copy(
                feats, feat_buf.at[v, mid], f_send.at[i, 0], f_recv.at[i, 0],
                device_id={"view": u}, device_id_type=MESH)
        if part == 1:
            return pltpu.make_async_remote_copy(
                feats.at[pl.ds(tokens_dev - edge, edge)], feat_buf.at[v, low],
                f_send.at[i, 1], f_recv.at[i, 1],
                device_id={"slab": s + 1, "view": u}, device_id_type=MESH)
        return pltpu.make_async_remote_copy(
            feats.at[pl.ds(0, edge)], feat_buf.at[v, high],
            f_send.at[i, 2], f_recv.at[i, 2],
            device_id={"slab": s - 1, "view": u}, device_id_type=MESH)

    own_feat = local(feats, feat_buf.at[v, mid], 0)

    def source_view(i):
        chip = lax.rem(v // 2 - i // 2 + n_view // 2, n_view // 2)
        return chip * 2 + lax.rem(half_id + i % 2, 2)

    def feat_landed(i, part):
        where = (mid, low, high)[part]
        ref = feat_buf.at[source_view(i), where]
        landed(None, lambda: ref, f_send.at[i, part], f_recv.at[i, part], view=source_view(1))

    for i in range(1, n_view):
        feat_copy(i, 0).start()

    @pl.when(s < n_slab - 1)
    def _():
        for i in range(n_view):
            feat_copy(i, 1).start()

    @pl.when(s > 0)
    def _():
        for i in range(n_view):
            feat_copy(i, 2).start()

    if gather:
        send_own(KV)
    loads = [
        local(stream, stream_buf, 1),
        local(queries, query_buf, 2),
        local(gain, gain_buf, 3),
    ]
    if gather:
        weight_loads = []
        for w in range(4):
            rows = srcs[w].shape[0]
            at = pl.ds(pl.multiple_of((d * n_slab + s) * rows, 16), rows)
            weight_loads.append(local(srcs[w], bufs[w].at[at], 4 + w))
    else:
        weight_loads = [local(srcs[w], bufs[w], 4 + w) for w in range(4)]

    @pl.when(s == 0)
    def _():
        feat_buf[:, 0:edge, :] = jnp.zeros((n_view, edge, channels), jnp.bfloat16)

    @pl.when(s == n_slab - 1)
    def _():
        feat_buf[:, edge + tokens_dev:, :] = jnp.zeros((n_view, edge, channels), jnp.bfloat16)

    k_count = n_view * near * col_count
    lane = lax.broadcasted_iota(jnp.int32, (1, k_count), 1)
    key_view = jnp.zeros((1, k_count), jnp.int32)
    key_row = jnp.zeros((1, k_count), jnp.int32)
    for b in range(1, n_view * near):
        key_row = key_row + jnp.where(lane >= b * col_count, 1, 0)
    for b in range(1, n_view):
        key_view = key_view + jnp.where(lane >= b * near * col_count, 1, 0)
    key_row = key_row - near * key_view + (s * row_count - HALO)
    seen = jnp.zeros((1, k_count), jnp.int32)
    for u in range(n_view):
        flag = jnp.where(v == u, 1, visible[0, v, u])
        seen = jnp.where(key_view == u, flag, seen)
    for r in range(row_count):
        first = jnp.zeros((1, k_count), jnp.int32)
        last = jnp.zeros((1, k_count), jnp.int32)
        for u in range(n_view):
            first = jnp.where(key_view == u, starts[0, 0, r, u], first)
            last = jnp.where(key_view == u, ends[0, 0, r, u], last)
        fits = jnp.where(key_row >= first, 1, 0) * jnp.where(key_row < last, 1, 0)
        fits = fits * jnp.where(seen == 1, 1, 0)
        addend = jnp.where(fits == 1, 0.0, -1e30)
        bias_buf[r * col_count:(r + 1) * col_count, :] = jnp.broadcast_to(
            addend, (col_count, k_count))

    if gather:
        for hop in range(1, n_slab):
            relay_z(CONV, hop)
            take_y(CONV, hop - 1)
            if hop == 1:
                send_own(UP)
            relay_z(KV, hop)
            take_y(KV, hop - 1)
        send_own(DOWN)
        take_y(CONV, n_slab - 1)
        take_y(KV, n_slab - 1)
    own_feat.wait()
    for i in range(1, n_view):
        feat_landed(i, 0)

    @pl.when(s > 0)
    def _():
        for i in range(n_view):
            feat_landed(i, 1)

    @pl.when(s < n_slab - 1)
    def _():
        for i in range(n_view):
            feat_landed(i, 2)

    weight_loads[CONV].wait()
    if gather:
        take_core(CONV)

    span = near * col_count
    count = (row_count + 2 * (HALO + 1)) * col_count
    column = lax.broadcasted_iota(jnp.int32, (count, channels), 0) & (col_count - 1)
    for u in range(n_view):
        x = feat_buf[u]
        wide = x.astype(jnp.float32)
        before = jnp.where(column == 0, 0.0, pltpu.roll(wide, 1, 0)).astype(jnp.bfloat16)
        after = jnp.where(column == col_count - 1, 0.0, pltpu.roll(wide, count - 1, 0)).astype(
            jnp.bfloat16)
        taps = [
            part[row * col_count:row * col_count + span]
            for row in range(3) for part in (before, x, after)
        ]
        running = jnp.dot(jnp.concatenate(taps, axis=1), conv_buf[...],
                          preferred_element_type=jnp.float32)
        gated = running / (1.0 + jnp.exp(-running))
        enc_buf[u * span:(u + 1) * span, :] = (
            wide[HALO * col_count:HALO * col_count + span] + gated).astype(jnp.bfloat16)

    weight_loads[KV].wait()
    if gather:
        relay_z(UP, 1)
        take_core(KV)
    for u in range(n_view):
        proj_buf[u * span:(u + 1) * span, :] = jnp.dot(
            enc_buf[u * span:(u + 1) * span, :], kv_buf[...],
            preferred_element_type=jnp.float32).astype(jnp.bfloat16)

    for copy in loads:
        copy.wait()

    per = 256 // HEAD_DIM
    head_of = lax.broadcasted_iota(jnp.int32, (tokens_dev, per * HEAD_DIM), 1) // HEAD_DIM
    total = jnp.zeros((tokens_dev, 1), jnp.float32)
    for g in range(width // (per * HEAD_DIM)):
        if gather and g + 2 < n_slab:
            relay_z(UP, g + 2)
        at = slice(g * per * HEAD_DIM, (g + 1) * per * HEAD_DIM)
        query = query_buf[:, at] * jnp.bfloat16(HEAD_DIM ** -0.5)
        stack = jnp.concatenate(
            [jnp.where(head_of == h, query, jnp.bfloat16(0)) for h in range(per)], axis=0)
        scores = lax.dot_general(stack, proj_buf[:, at], (((1,), (1,)), ((), ())),
                                 preferred_element_type=jnp.float32)
        value = proj_buf[:, width + g * per * HEAD_DIM:width + (g + 1) * per * HEAD_DIM]
        attended = jnp.zeros((tokens_dev, per * HEAD_DIM), jnp.float32)
        for h in range(per):
            part = scores[h * tokens_dev:(h + 1) * tokens_dev] + bias_buf[...]
            weights = jnp.exp(part - jnp.max(part, axis=1, keepdims=True))
            inverse = 1.0 / jnp.sum(weights, axis=1, keepdims=True)
            probs = (weights * inverse).astype(jnp.bfloat16)
            mixed = jnp.dot(probs, value, preferred_element_type=jnp.float32)
            attended = jnp.where(head_of == h, mixed, attended)
        residual = stream_buf[:, at].astype(jnp.float32) + attended
        res_buf[:, at] = residual
        total = total + jnp.sum(residual * residual, axis=1, keepdims=True)
    scale = lax.rsqrt(total * (1.0 / width) + 1e-06)
    tokens[v] = (res_buf[...] * scale * gain_buf[...][None, :]).astype(jnp.bfloat16)
    for i in [1] + list(range(2, n_view, 2)):
        push(None, lambda: tokens.at[v], lambda: tokens.at[v], t_send.at[i], t_recv.at[i],
             view=view_at(i))
    if gather:
        for hop in range(width // (per * HEAD_DIM) + 2, n_slab):
            relay_z(UP, hop)
        for hop in range(1, n_slab):
            relay_z(DOWN, hop)
        for hop in range(n_slab):
            take_y(UP, hop)
    weight_loads[UP].wait()

    def unit(u):
        return jax.nn.gelu(
            jnp.dot(tokens[u], up_buf[...], preferred_element_type=jnp.float32),
            approximate=True).astype(jnp.bfloat16)

    def term(hidden):
        return lax.dot_general(hidden, down_buf[...], (((1,), (1,)), ((), ())),
                               preferred_element_type=jnp.float32).astype(jnp.bfloat16)

    def take_tokens(i):
        landed(None, lambda: tokens.at[source_view(i)], t_send.at[i], t_recv.at[i],
               view=source_view(i))

    hidden = {0: unit(v)}
    take_tokens(1)
    hidden[1] = unit(partner)
    for i in range(2, n_view, 2):
        take_tokens(i)
        part = lambda i=i: tokens.at[source_view(i)]
        push(None, part, part, t_send.at[i + 1], t_recv.at[i + 1], view=partner)
    for i in range(2, n_view, 2):
        hidden[i] = unit(source_view(i))
        take_tokens(i + 1)
        hidden[i + 1] = unit(source_view(i + 1))
    weight_loads[DOWN].wait()
    if gather:
        for hop in range(n_slab):
            take_y(DOWN, hop)
    for i in range(2, n_view, 2):
        terms[i + 1] = term(hidden[i + 1])
        push(None, lambda i=i: terms.at[i + 1], lambda i=i: sums.at[i + 1], s_send.at[i + 1],
             s_recv.at[i + 1], view=partner)
    for i in range(2, n_view, 2):
        mine = term(hidden[i]).astype(jnp.float32)
        landed(None, lambda: sums.at[i + 1], s_send.at[i + 1], s_recv.at[i + 1], view=partner)
        terms[i] = (mine + sums[i + 1].astype(jnp.float32)).astype(jnp.bfloat16)
        push(None, lambda i=i: terms.at[i], lambda i=i: sums.at[i], s_send.at[i], s_recv.at[i],
             view=source_view(i))
    terms[1] = term(hidden[1])
    push(None, lambda: terms.at[1], lambda: sums.at[1], s_send.at[1], s_recv.at[1], view=partner)
    mixed = term(hidden[0]).astype(jnp.float32)
    for i in [1] + list(range(2, n_view, 2)):
        landed(None, lambda: sums.at[i], s_send.at[i], s_recv.at[i], view=view_at(i))
        mixed = mixed + sums[i].astype(jnp.float32)
    out[...] = (res_buf[...] + mixed).astype(jnp.bfloat16)

    for cond, copy in sends:
        only(cond, lambda: copy().wait_send())
    for i in range(1, n_view):
        feat_copy(i, 0).wait_send()

    @pl.when(s < n_slab - 1)
    def _():
        for i in range(n_view):
            feat_copy(i, 1).wait_send()

    @pl.when(s > 0)
    def _():
        for i in range(n_view):
            feat_copy(i, 2).wait_send()


def solution(mesh):
    n_dp, n_slab, n_view = (mesh.shape[name] for name in ("dp", "slab", "view"))

    def shards(
        latent_feats, conv_weight, kv_weight, stream, queries, norm_gain,
        up_weight, down_weight, band_start, band_end, visibility,
    ):
        row_count, col_count, channels = latent_feats.shape[2:]
        width = stream.shape[4]
        units = up_weight.shape[1]
        tokens = row_count * col_count
        group = n_dp * n_slab
        weights = [conv_weight, kv_weight, up_weight, down_weight]
        gather = all(w.shape[0] % 16 == 0 for w in weights)
        if not gather:
            weights = [lax.all_gather(w, ("dp", "slab"), axis=0, tiled=True) for w in weights]
        near = row_count + 2 * HALO
        count = row_count + 2 * (HALO + 1)
        keys = n_view * near * col_count

        def kernel(*refs):
            block_kernel(n_dp, n_slab, n_view, gather, row_count, col_count, *refs)

        anywhere = pl.BlockSpec(memory_space=pl.ANY)
        scalar = pl.BlockSpec(memory_space=pltpu.SMEM)
        half = jnp.bfloat16
        dma = pltpu.SemaphoreType.DMA
        result = pl.pallas_call(
            kernel,
            out_shape=jax.ShapeDtypeStruct((tokens, width), half),
            in_specs=[anywhere] * 8 + [scalar] * 3,
            out_specs=pl.BlockSpec(memory_space=pltpu.VMEM),
            scratch_shapes=[
                pltpu.VMEM((9 * channels, channels), half),
                pltpu.VMEM((channels, 2 * width), half),
                pltpu.VMEM((width, units), half),
                pltpu.VMEM((width, units), half),
                pltpu.VMEM((n_view, count * col_count, channels), half),
                pltpu.VMEM((keys, channels), half),
                pltpu.VMEM((keys, 2 * width), half),
                pltpu.VMEM((tokens, keys), jnp.float32),
                pltpu.VMEM((tokens, width), half),
                pltpu.VMEM((tokens, width), half),
                pltpu.VMEM((width,), jnp.float32),
                pltpu.VMEM((tokens, width), jnp.float32),
                pltpu.VMEM((n_view, tokens, width), half),
                pltpu.VMEM((n_view, tokens, width), half),
                pltpu.VMEM((n_view, tokens, width), half),
                dma((8,)),
                dma((4, 2, n_slab)), dma((4, 2, n_slab)),
                dma((4, n_dp, 2, n_slab)), dma((4, n_dp, 2, n_slab)),
                dma((2, n_dp, 2, n_slab)), dma((2, n_dp, 2, n_slab)),
                dma((n_view, 3)), dma((n_view, 3)),
                dma((n_view,)), dma((n_view,)),
                dma((n_view,)), dma((n_view,)),
            ],
            compiler_params=pltpu.CompilerParams(collective_id=0, has_side_effects=True),
        )(
            latent_feats.reshape(tokens, channels), weights[0], weights[1],
            stream.reshape(tokens, width), queries.reshape(tokens, width),
            norm_gain, weights[2], weights[3],
            band_start, band_end, visibility,
        )
        return result.reshape(1, 1, row_count, col_count, width)

    return jax.shard_map(
        shards,
        mesh=mesh,
        in_specs=(
            P("dp", "view", "slab", None, None),
            P(("dp", "slab"), None),
            P(("dp", "slab"), None),
            P("dp", "view", "slab", None, None),
            P("dp", "view", "slab", None, None),
            P(),
            P(("dp", "slab"), "view"),
            P(("dp", "slab"), "view"),
            P("dp", "view", "slab", None),
            P("dp", "view", "slab", None),
            P("dp", None, None),
        ),
        out_specs=P("dp", "view", "slab", None, None),
        check_vma=False,
    )
```
